256 devices in a mesh: row: 8 (over x, core), col: 32 (over z, y).
Axes of the slice: x: 4, y: 4, z: 8, core: 2. Of those that a mesh axis runs over, the one named last changes fastest.
Arguments:
- query_weight: float32 [16384, 16384], P('row', 'col'), may hold values from -6 to 6
Outputs:
- rotated: float32 [16384, 16384], P('row', 'col')
The draws below stay inside these ranges and needn't reach their ends.
All inputs are finite; a program needn't handle non-finite values.
Results may differ from the reference program's by a relative error of at most 0.0001.
Values sent between devices are 32-bit elements; how exact they have to be, the bound alone decides.
A program may use at most 128 MiB of HBM per device.

```python
import jax
import jax.numpy as jnp
from jax import lax

D = 16384


def block_scale(stream_key, shape, cuts, low, largest):
    gain = 1.0
    for dim, blocks in cuts:
        draws = jax.random.uniform(jax.random.fold_in(jax.random.fold_in(stream_key, 6), dim), (blocks,), jnp.float32, low / len(cuts), largest / len(cuts))
        gain = gain * jnp.repeat(jnp.exp(draws), shape[dim] // blocks).reshape((-1,) + (1,) * (len(shape) - 1 - dim))
    return gain


def gaussian(own_key, extent, spread, most, pieces=(), kind=jnp.bfloat16):
    values = jax.random.normal(own_key, extent, jnp.float32) * spread
    if len(pieces) > 0:
        values = block_scale(own_key, extent, pieces, -0.22, 0.18) * values
    return jnp.clip(values, min=-most, max=most).astype(kind)


def setup_inputs(seed: int = 0) -> dict:
    streams_of = jax.random.split(jax.random.key(seed), 2)
    query_weight = gaussian(streams_of[0], (D, D), 1.0, 6.0, ((0, 8), (1, 32)), jnp.float32)
    return {"query_weight": query_weight}


def hadamard_table(length):
    rows_idx = lax.broadcasted_iota(jnp.int32, (length, length), 0)
    cols_idx = lax.broadcasted_iota(jnp.int32, (length, length), 1)
    common_bits = jnp.bitwise_and(rows_idx, cols_idx)
    parity = jnp.zeros((length, length), jnp.int32)
    for bit_pos in range(length.bit_length() - 1):
        parity = parity + jnp.bitwise_and(jnp.right_shift(common_bits, bit_pos), 1)
    return (1 - 2 * jnp.bitwise_and(parity, 1)).astype(jnp.float32)


def split_length(length):
    factors = []
    remain = length
    while remain > 128:
        factors.append(128)
        remain = remain // 128
    factors.append(remain)
    return factors


def transform_axis(values, along):
    factors = split_length(values.shape[along])
    shaped = values.reshape(values.shape[:along] + tuple(factors) + values.shape[along + 1:])
    letters = "abcdefghij"
    rank_all = shaped.ndim
    for offset, factor in enumerate(factors):
        place = along + offset
        source = letters[:rank_all]
        target = source[:place] + "z" + source[place + 1:]
        signs = hadamard_table(factor).astype(values.dtype)
        shaped = jnp.einsum("z" + source[place] + "," + source + "->" + target, signs, shaped, precision=lax.Precision.HIGHEST)
    return shaped.reshape(values.shape)


def reference(query_weight):
    left = transform_axis(query_weight, 0)
    return transform_axis(left, 1) * (1.0 / D)
```

```python
import functools

import jax
import jax.numpy as jnp
from jax import lax
from jax.experimental import pallas as pl
from jax.experimental.pallas import tpu as pltpu
from jax.sharding import PartitionSpec as P

MESH = pl.DeviceIdType.MESH
LANES = 128
CHUNKS = 4
Z_ORDER = (1, 7, 2, 6, 3, 5, 4)


def butterfly(values):
    values = list(values)
    half = 1
    while half < len(values):
        for base in range(0, len(values), 2 * half):
            for i in range(base, base + half):
                low, high = values[i], values[i + half]
                values[i], values[i + half] = low + high, low - high
        half *= 2
    return values


def signs(rows, cols):
    i = lax.broadcasted_iota(jnp.int32, (rows, cols), 0)
    j = lax.broadcasted_iota(jnp.int32, (rows, cols), 1)
    bits = jnp.bitwise_and(i, j)
    for shift in (8, 4, 2, 1):
        bits = jnp.bitwise_xor(bits, jnp.right_shift(bits, shift))
    return (1 - 2 * jnp.bitwise_and(bits, 1)).astype(jnp.float32).astype(jnp.bfloat16)


def split(value):
    high = value.astype(jnp.bfloat16)
    low = (value - high.astype(jnp.float32)).astype(jnp.bfloat16)
    return high, low


def exchange_kernel(n_z, n_y, n_row, x_ref, a_out, b_out, z_in, z_sum, z_back, p_in, p_sum, p_back, local, table, send_sem, recv_sem, out_sem):
    row = lax.axis_index("row")
    col = lax.axis_index("col")
    z = col // n_y
    y = lax.rem(col, n_y)
    n_p = n_row * n_y
    p = row * n_y + y
    blocks, lanes = x_ref.shape[1], x_ref.shape[3]
    z_len, p_len = blocks // n_z, blocks // n_p

    def z_peer(step):
        k = lax.rem(z + step, n_z)
        return k, (row, k * n_y + y)

    def p_peer(step):
        k = lax.rem(p + step, n_p)
        return k, (k // n_y, z * n_y + lax.rem(k, n_y))

    barrier = pltpu.get_barrier_semaphore()
    for step in Z_ORDER:
        pl.semaphore_signal(barrier, inc=1, device_id=z_peer(step)[1], device_id_type=MESH)

    @pl.loop(1, n_p)
    def _(step):
        pl.semaphore_signal(barrier, inc=1, device_id=p_peer(step)[1], device_id_type=MESH)

    pl.semaphore_wait(barrier, n_z - 1 + n_p - 1)

    def z_send(src, dst, slot):
        mine = pl.ds(z * z_len, z_len)
        for step in Z_ORDER:
            k, device = z_peer(step)
            pltpu.make_async_remote_copy(
                src_ref=src.at[pl.ds(k * z_len, z_len)], dst_ref=dst.at[mine],
                send_sem=send_sem.at[slot], recv_sem=recv_sem.at[slot], device_id=device, device_id_type=MESH,
            ).start()
        pltpu.make_async_copy(src.at[mine], dst.at[mine], recv_sem.at[slot]).start()

    def p_send(src, dst, slot):
        mine = pl.ds(p * p_len, p_len)

        @pl.loop(1, n_p)
        def _(step):
            k, device = p_peer(step)
            pltpu.make_async_remote_copy(
                src_ref=src.at[pl.ds(k * p_len, p_len)], dst_ref=dst.at[mine],
                send_sem=send_sem.at[slot], recv_sem=recv_sem.at[slot], device_id=device, device_id_type=MESH,
            ).start()

        pltpu.make_async_copy(src.at[mine], dst.at[mine], recv_sem.at[slot]).start()

    def arrived(dst, slot):
        pltpu.make_async_copy(dst, dst, recv_sem.at[slot]).wait()

    def sent(ref, length, slot):
        part = ref.at[pl.ds(0, blocks - length)]
        pltpu.make_async_copy(part, part, send_sem.at[slot]).wait()

    def combine(src, dst, count, length):
        @pl.loop(0, length)
        def _(t):
            for lane in range(0, lanes, LANES):
                at = slice(lane, lane + LANES)
                done = butterfly([src[k * length + t, :, at] for k in range(count)])
                for k in range(count):
                    dst[k * length + t, :, at] = done[k]

    def transform(src, dst):
        size = 256
        groups = blocks * 8 // size
        step_blocks = size // 8

        @pl.loop(0, 2 * groups)
        def _(g):
            chunk, part = g // groups, lax.rem(g, groups)
            at = pl.ds(part * step_blocks, step_blocks)
            high, low = split(src[chunk, at].reshape(size, lanes))
            wide = table[...]
            value = jnp.dot(high, wide, preferred_element_type=jnp.float32) + jnp.dot(low, wide, preferred_element_type=jnp.float32)
            high, low = split(value)
            tall = table[0:size, 0:size]
            value = jnp.dot(tall, high, preferred_element_type=jnp.float32) + jnp.dot(tall, low, preferred_element_type=jnp.float32)
            dst[chunk, at] = value.reshape(step_blocks, 8, lanes)

        @pl.loop(0, step_blocks)
        def _(t):
            for lane in range(0, lanes, LANES):
                at = slice(lane, lane + LANES)
                places = [(chunk, part * step_blocks) for chunk in range(2) for part in range(groups)]
                done = butterfly([dst[chunk, base + t, :, at] for chunk, base in places])
                for (chunk, base), value in zip(places, done):
                    dst[chunk, base + t, :, at] = value

    a_chunks, b_chunks = (0, 1), (2, 3)
    for a, b in zip(a_chunks, b_chunks):
        z_send(x_ref.at[a], z_in.at[a], a)
        p_send(x_ref.at[b], p_in.at[b], 8 + b)

    table[...] = signs(lanes, lanes)

    for a, b in zip(a_chunks, b_chunks):
        arrived(p_in.at[b], 8 + b)
        combine(p_in.at[b], p_sum.at[b], n_p, p_len)
        p_send(p_sum.at[b], p_back.at[b], 12 + b)
        arrived(z_in.at[a], a)
        combine(z_in.at[a], z_sum.at[a], n_z, z_len)
        z_send(z_sum.at[a], z_back.at[a], 4 + a)

    for b in b_chunks:
        arrived(p_back.at[b], 12 + b)
    transform(p_back.at[pl.ds(2, 2)], local.at[pl.ds(2, 2)])
    for b in b_chunks:
        z_send(local.at[b], z_in.at[b], b)

    for a in a_chunks:
        arrived(z_back.at[a], 4 + a)
        p_send(z_back.at[a], p_in.at[a], 8 + a)
    for a in a_chunks:
        arrived(p_in.at[a], 8 + a)
        combine(p_in.at[a], p_sum.at[a], n_p, p_len)
        p_send(p_sum.at[a], p_back.at[a], 12 + a)

    arrived(z_in.at[2], 2)
    combine(z_in.at[2], z_sum.at[2], n_z, z_len)
    z_send(z_sum.at[2], b_out.at[0], 6)

    for a in a_chunks:
        arrived(p_back.at[a], 12 + a)
    transform(p_back.at[pl.ds(0, 2)], local.at[pl.ds(0, 2)])
    pltpu.make_async_copy(local.at[pl.ds(0, 2)], a_out, out_sem).start()

    arrived(z_in.at[3], 3)
    combine(z_in.at[3], z_sum.at[3], n_z, z_len)
    z_send(z_sum.at[3], b_out.at[1], 7)

    for b in b_chunks:
        arrived(b_out.at[b - 2], 4 + b)
    pltpu.make_async_copy(local.at[pl.ds(0, 2)], a_out, out_sem).wait()
    for c in range(CHUNKS):
        sent(z_in.at[c], z_len, c)
        sent(z_in.at[c], z_len, 4 + c)
        sent(p_in.at[c], p_len, 8 + c)
        sent(p_in.at[c], p_len, 12 + c)


def mix_kernel(scale, a_ref, b_ref, o_ref):
    a, b = a_ref[...], b_ref[...]
    o_ref[0] = (a + b) * scale
    o_ref[1] = (a - b) * scale


def per_device(n_z, n_y, n_row, scale, query_weight):
    rows, lanes = query_weight.shape
    blocks = rows // CHUNKS // 8
    x = query_weight.reshape(CHUNKS, blocks, 8, lanes)
    half = jax.ShapeDtypeStruct((2, blocks, 8, lanes), jnp.float32)
    full = pltpu.VMEM((CHUNKS, blocks, 8, lanes), jnp.float32)
    anywhere = pl.BlockSpec(memory_space=pl.ANY)
    a, b = pl.pallas_call(
        functools.partial(exchange_kernel, n_z, n_y, n_row),
        out_shape=(half, half),
        in_specs=[anywhere],
        out_specs=(anywhere, anywhere),
        scratch_shapes=[
            full, full, pltpu.VMEM((2, blocks, 8, lanes), jnp.float32), full, full, full, full,
            pltpu.VMEM((lanes, lanes), jnp.bfloat16),
            pltpu.SemaphoreType.DMA((4 * CHUNKS,)), pltpu.SemaphoreType.DMA((4 * CHUNKS,)), pltpu.SemaphoreType.DMA,
        ],
        compiler_params=pltpu.CompilerParams(collective_id=0, has_side_effects=True, vmem_limit_bytes=60 * 2**20),
        name="exchange",
    )(x)
    steps = 4
    tall = rows // 2 // steps
    a, b = a.reshape(rows // 2, lanes), b.reshape(rows // 2, lanes)
    out = pl.pallas_call(
        functools.partial(mix_kernel, scale),
        out_shape=jax.ShapeDtypeStruct((2, rows // 2, lanes), jnp.float32),
        grid=(steps,),
        in_specs=[pl.BlockSpec((tall, lanes), lambda i: (i, 0))] * 2,
        out_specs=pl.BlockSpec((2, tall, lanes), lambda i: (0, i, 0)),
        name="mix",
    )(a, b)
    return out.reshape(rows, lanes)


def solution(mesh):
    n_row, n_col = mesh.shape["row"], mesh.shape["col"]
    n_y = 4
    n_z = n_col // n_y

    def run(query_weight):
        scale = 1.0 / query_weight.shape[0]
        body = functools.partial(per_device, n_z, n_y, n_row, scale)
        return jax.shard_map(body, mesh=mesh, in_specs=(P("row", "col"),), out_specs=P("row", "col"), check_vma=False)(query_weight)

    return run
```

```python
import functools

import jax
import jax.numpy as jnp
from jax import lax
from jax.experimental import pallas as pl
from jax.experimental.pallas import tpu as pltpu
from jax.sharding import PartitionSpec as P

MESH = pl.DeviceIdType.MESH
LANES = 128
CHUNKS = 4
Z_ORDER = (4, 3, 5, 2, 6, 1, 7)


def butterfly(values):
    values = list(values)
    half = 1
    while half < len(values):
        for base in range(0, len(values), 2 * half):
            for i in range(base, base + half):
                low, high = values[i], values[i + half]
                values[i], values[i + half] = low + high, low - high
        half *= 2
    return values


def signs(rows, cols):
    i = lax.broadcasted_iota(jnp.int32, (rows, cols), 0)
    j = lax.broadcasted_iota(jnp.int32, (rows, cols), 1)
    bits = jnp.bitwise_and(i, j)
    for shift in (8, 4, 2, 1):
        bits = jnp.bitwise_xor(bits, jnp.right_shift(bits, shift))
    return (1 - 2 * jnp.bitwise_and(bits, 1)).astype(jnp.float32).astype(jnp.bfloat16)


def split(value):
    high = value.astype(jnp.bfloat16)
    low = (value - high.astype(jnp.float32)).astype(jnp.bfloat16)
    return high, low


def exchange_kernel(n_z, n_y, n_row, x_ref, a_out, b_out, z_in, z_sum, z_back, p_in, p_sum, p_back, local, table, send_sem, recv_sem):
    row = lax.axis_index("row")
    col = lax.axis_index("col")
    z = col // n_y
    y = lax.rem(col, n_y)
    n_p = n_row * n_y
    p = row * n_y + y
    blocks, lanes = x_ref.shape[1], x_ref.shape[3]
    z_len, p_len = blocks // n_z, blocks // n_p

    def z_peer(step):
        k = lax.rem(z + step, n_z)
        return k, (row, k * n_y + y)

    def p_peer(step):
        k = lax.rem(p + step, n_p)
        return k, (k // n_y, z * n_y + lax.rem(k, n_y))

    barrier = pltpu.get_barrier_semaphore()
    for step in Z_ORDER:
        pl.semaphore_signal(barrier, inc=1, device_id=z_peer(step)[1], device_id_type=MESH)

    @pl.loop(1, n_p)
    def _(step):
        pl.semaphore_signal(barrier, inc=1, device_id=p_peer(step)[1], device_id_type=MESH)

    pl.semaphore_wait(barrier, n_z - 1 + n_p - 1)

    def z_send(src, dst, slot):
        mine = pl.ds(z * z_len, z_len)
        for step in Z_ORDER:
            k, device = z_peer(step)
            pltpu.make_async_remote_copy(
                src_ref=src.at[pl.ds(k * z_len, z_len)], dst_ref=dst.at[mine],
                send_sem=send_sem.at[slot], recv_sem=recv_sem.at[slot], device_id=device, device_id_type=MESH,
            ).start()
        pltpu.make_async_copy(src.at[mine], dst.at[mine], recv_sem.at[slot]).start()

    def p_send(src, dst, slot):
        mine = pl.ds(p * p_len, p_len)

        @pl.loop(1, n_p)
        def _(step):
            k, device = p_peer(step)
            pltpu.make_async_remote_copy(
                src_ref=src.at[pl.ds(k * p_len, p_len)], dst_ref=dst.at[mine],
                send_sem=send_sem.at[slot], recv_sem=recv_sem.at[slot], device_id=device, device_id_type=MESH,
            ).start()

        pltpu.make_async_copy(src.at[mine], dst.at[mine], recv_sem.at[slot]).start()

    def arrived(dst, slot):
        pltpu.make_async_copy(dst, dst, recv_sem.at[slot]).wait()

    def sent(ref, length, slot):
        part = ref.at[pl.ds(0, blocks - length)]
        pltpu.make_async_copy(part, part, send_sem.at[slot]).wait()

    def combine(src, dst, count, length):
        @pl.loop(0, length)
        def _(t):
            for lane in range(0, lanes, LANES):
                at = slice(lane, lane + LANES)
                done = butterfly([src[k * length + t, :, at] for k in range(count)])
                for k in range(count):
                    dst[k * length + t, :, at] = done[k]

    def transform(src, dst):
        size = 256
        groups = blocks * 8 // size
        step_blocks = size // 8

        @pl.loop(0, 2 * groups)
        def _(g):
            chunk, part = g // groups, lax.rem(g, groups)
            at = pl.ds(part * step_blocks, step_blocks)
            high, low = split(src[chunk, at].reshape(size, lanes))
            wide = table[...]
            value = jnp.dot(high, wide, preferred_element_type=jnp.float32) + jnp.dot(low, wide, preferred_element_type=jnp.float32)
            high, low = split(value)
            tall = table[0:size, 0:size]
            value = jnp.dot(tall, high, preferred_element_type=jnp.float32) + jnp.dot(tall, low, preferred_element_type=jnp.float32)
            dst[chunk, at] = value.reshape(step_blocks, 8, lanes)

        @pl.loop(0, step_blocks)
        def _(t):
            for lane in range(0, lanes, LANES):
                at = slice(lane, lane + LANES)
                places = [(chunk, part * step_blocks) for chunk in range(2) for part in range(groups)]
                done = butterfly([dst[chunk, base + t, :, at] for chunk, base in places])
                for (chunk, base), value in zip(places, done):
                    dst[chunk, base + t, :, at] = value

    a_chunks, b_chunks = (0, 1), (2, 3)
    for a, b in zip(a_chunks, b_chunks):
        z_send(x_ref.at[a], z_in.at[a], a)
        p_send(x_ref.at[b], p_in.at[b], 8 + b)

    table[...] = signs(lanes, lanes)

    for a, b in zip(a_chunks, b_chunks):
        arrived(p_in.at[b], 8 + b)
        combine(p_in.at[b], p_sum.at[b], n_p, p_len)
        p_send(p_sum.at[b], p_back.at[b], 12 + b)
        arrived(z_in.at[a], a)
        combine(z_in.at[a], z_sum.at[a], n_z, z_len)
        z_send(z_sum.at[a], z_back.at[a], 4 + a)

    for b in b_chunks:
        arrived(p_back.at[b], 12 + b)
    transform(p_back.at[pl.ds(2, 2)], local)
    for b in b_chunks:
        z_send(local.at[b - 2], z_in.at[b], b)

    for a in a_chunks:
        arrived(z_back.at[a], 4 + a)
        p_send(z_back.at[a], p_in.at[a], 8 + a)
    for a in a_chunks:
        arrived(p_in.at[a], 8 + a)
        combine(p_in.at[a], p_sum.at[a], n_p, p_len)
        p_send(p_sum.at[a], p_back.at[a], 12 + a)

    arrived(z_in.at[2], 2)
    combine(z_in.at[2], z_sum.at[2], n_z, z_len)
    z_send(z_sum.at[2], b_out.at[0], 6)

    for a in a_chunks:
        arrived(p_back.at[a], 12 + a)
    transform(p_back.at[pl.ds(0, 2)], a_out)

    arrived(z_in.at[3], 3)
    combine(z_in.at[3], z_sum.at[3], n_z, z_len)
    z_send(z_sum.at[3], b_out.at[1], 7)

    for b in b_chunks:
        arrived(b_out.at[b - 2], 4 + b)
    for c in range(CHUNKS):
        sent(z_in.at[c], z_len, c)
        sent(z_in.at[c], z_len, 4 + c)
        sent(p_in.at[c], p_len, 8 + c)
        sent(p_in.at[c], p_len, 12 + c)


def mix_kernel(scale, steps, a_ref, b_ref, o_ref, plus, minus, sem):
    chunks, blocks = a_ref.shape[:2]
    size = chunks * blocks // steps
    copies = []
    for i in range(steps):
        chunk, at = i * size // blocks, pl.ds(i * size % blocks, size)
        a, b = a_ref[chunk, at], b_ref[chunk, at]
        plus[chunk, at] = (a + b) * scale
        minus[chunk, at] = (a - b) * scale
        for half, made in enumerate((plus, minus)):
            copies.append(pltpu.make_async_copy(made.at[chunk, at], o_ref.at[half, chunk, at], sem.at[half, i]))
            copies[-1].start()
    for copy in copies:
        copy.wait()


def per_device(n_z, n_y, n_row, scale, query_weight):
    rows, lanes = query_weight.shape
    blocks = rows // CHUNKS // 8
    x = query_weight.reshape(CHUNKS, blocks, 8, lanes)
    half = pltpu.VMEM((2, blocks, 8, lanes), jnp.float32)
    full = pltpu.VMEM((CHUNKS, blocks, 8, lanes), jnp.float32)
    anywhere = pl.BlockSpec(memory_space=pl.ANY)
    a, b = pl.pallas_call(
        functools.partial(exchange_kernel, n_z, n_y, n_row),
        out_shape=(half, half),
        in_specs=[pl.BlockSpec(memory_space=pltpu.HBM)],
        out_specs=(pl.BlockSpec(memory_space=pltpu.VMEM),) * 2,
        scratch_shapes=[
            full, full, half, full, full, full, half,
            pltpu.VMEM((lanes, lanes), jnp.bfloat16),
            pltpu.SemaphoreType.DMA((4 * CHUNKS,)), pltpu.SemaphoreType.DMA((4 * CHUNKS,)),
        ],
        compiler_params=pltpu.CompilerParams(collective_id=0, has_side_effects=True, vmem_limit_bytes=58 * 2**20),
        name="exchange",
    )(x)
    steps = 8
    a, b = (pltpu.with_memory_space_constraint(part, pltpu.VMEM) for part in (a, b))
    out = pl.pallas_call(
        functools.partial(mix_kernel, scale, steps),
        out_shape=jax.ShapeDtypeStruct((2, *half.shape), jnp.float32),
        in_specs=[pl.BlockSpec(memory_space=pltpu.VMEM)] * 2,
        out_specs=anywhere,
        scratch_shapes=[half, half, pltpu.SemaphoreType.DMA((2, steps))],
        compiler_params=pltpu.CompilerParams(vmem_limit_bytes=16 * 2**20),
        name="mix",
    )(a, b)
    return out.reshape(rows, lanes)


def solution(mesh):
    n_row, n_col = mesh.shape["row"], mesh.shape["col"]
    n_y = 4
    n_z = n_col // n_y

    def run(query_weight):
        scale = 1.0 / query_weight.shape[0]
        body = functools.partial(per_device, n_z, n_y, n_row, scale)
        return jax.shard_map(body, mesh=mesh, in_specs=(P("row", "col"),), out_specs=P("row", "col"), check_vma=False)(query_weight)

    return run
```

```python
import functools

import jax
import jax.numpy as jnp
from jax import lax
from jax.experimental import pallas as pl
from jax.experimental.pallas import tpu as pltpu
from jax.sharding import PartitionSpec as P

MESH = pl.DeviceIdType.MESH
LANES = 128
CHUNKS = 4
Z_FAR = (4, 3, 5)
Z_NEAR = (2, 6, 1, 7)


def butterfly(values):
    values = list(values)
    half = 1
    while half < len(values):
        for base in range(0, len(values), 2 * half):
            for i in range(base, base + half):
                low, high = values[i], values[i + half]
                values[i], values[i + half] = low + high, low - high
        half *= 2
    return values


def signs(rows, cols):
    i = lax.broadcasted_iota(jnp.int32, (rows, cols), 0)
    j = lax.broadcasted_iota(jnp.int32, (rows, cols), 1)
    bits = jnp.bitwise_and(i, j)
    for shift in (8, 4, 2, 1):
        bits = jnp.bitwise_xor(bits, jnp.right_shift(bits, shift))
    return (1 - 2 * jnp.bitwise_and(bits, 1)).astype(jnp.float32).astype(jnp.bfloat16)


def split(value):
    high = value.astype(jnp.bfloat16)
    low = (value - high.astype(jnp.float32)).astype(jnp.bfloat16)
    return high, low


def exchange_kernel(n_z, n_y, n_row, x_ref, a_out, b_out, z_in, z_sum, z_back, p_in, p_sum, p_back, local, table, send_sem, recv_sem, ready_sem):
    row = lax.axis_index("row")
    col = lax.axis_index("col")
    z = col // n_y
    y = lax.rem(col, n_y)
    n_p = n_row * n_y
    p = row * n_y + y
    blocks, lanes = x_ref.shape[1], x_ref.shape[3]
    z_len, p_len = blocks // n_z, blocks // n_p

    def z_peer(step):
        k = lax.rem(z + step, n_z)
        return k, (row, k * n_y + y)

    def p_peer(step):
        k = lax.rem(p + step, n_p)
        return k, (k // n_y, z * n_y + lax.rem(k, n_y))

    x, core = row // 2, lax.rem(row, 2)
    n_x = n_row // 2
    neighbours = [z_peer(1)[1], z_peer(n_z - 1)[1]]
    neighbours += [(row, z * n_y + lax.rem(y + step, n_y)) for step in (1, n_y - 1)]
    neighbours += [(lax.rem(x + step, n_x) * 2 + core, col) for step in (1, n_x - 1)]
    neighbours += [(x * 2 + 1 - core, col)]

    def greet(semaphore):
        for device in neighbours:
            pl.semaphore_signal(semaphore, inc=1, device_id=device, device_id_type=MESH)
        pl.semaphore_wait(semaphore, len(neighbours))

    def z_pieces(src, dst, slot, steps):
        mine = pl.ds(z * z_len, z_len)
        for step in steps:
            k, device = z_peer(step)
            pltpu.make_async_remote_copy(
                src_ref=src.at[pl.ds(k * z_len, z_len)], dst_ref=dst.at[mine],
                send_sem=send_sem.at[slot], recv_sem=recv_sem.at[slot], device_id=device, device_id_type=MESH,
            ).start()

    def z_own(src, dst, slot):
        mine = pl.ds(z * z_len, z_len)
        pltpu.make_async_copy(src.at[mine], dst.at[mine], recv_sem.at[slot]).start()

    def z_send(src, dst, slot, near=Z_NEAR):
        z_pieces(src, dst, slot, Z_FAR + near)
        z_own(src, dst, slot)

    def p_send(src, dst, slot):
        mine = pl.ds(p * p_len, p_len)

        @pl.loop(1, n_p)
        def _(step):
            k, device = p_peer(step)
            pltpu.make_async_remote_copy(
                src_ref=src.at[pl.ds(k * p_len, p_len)], dst_ref=dst.at[mine],
                send_sem=send_sem.at[slot], recv_sem=recv_sem.at[slot], device_id=device, device_id_type=MESH,
            ).start()

        pltpu.make_async_copy(src.at[mine], dst.at[mine], recv_sem.at[slot]).start()

    def arrived(dst, slot):
        pltpu.make_async_copy(dst, dst, recv_sem.at[slot]).wait()

    def sent(ref, length, slot):
        part = ref.at[pl.ds(0, blocks - length)]
        pltpu.make_async_copy(part, part, send_sem.at[slot]).wait()

    def combine(src, dst, count, length):
        @pl.loop(0, length)
        def _(t):
            for lane in range(0, lanes, LANES):
                at = slice(lane, lane + LANES)
                done = butterfly([src[k * length + t, :, at] for k in range(count)])
                for k in range(count):
                    dst[k * length + t, :, at] = done[k]

    def transform(src, dst):
        size = 256
        groups = blocks * 8 // size
        step_blocks = size // 8

        @pl.loop(0, 2 * groups)
        def _(g):
            chunk, part = g // groups, lax.rem(g, groups)
            at = pl.ds(part * step_blocks, step_blocks)
            high, low = split(src[chunk, at].reshape(size, lanes))
            wide = table[...]
            value = jnp.dot(high, wide, preferred_element_type=jnp.float32) + jnp.dot(low, wide, preferred_element_type=jnp.float32)
            high, low = split(value)
            tall = table[0:size, 0:size]
            value = jnp.dot(tall, high, preferred_element_type=jnp.float32) + jnp.dot(tall, low, preferred_element_type=jnp.float32)
            dst[chunk, at] = value.reshape(step_blocks, 8, lanes)

        @pl.loop(0, step_blocks)
        def _(t):
            for lane in range(0, lanes, LANES):
                at = slice(lane, lane + LANES)
                places = [(chunk, part * step_blocks) for chunk in range(2) for part in range(groups)]
                done = butterfly([dst[chunk, base + t, :, at] for chunk, base in places])
                for (chunk, base), value in zip(places, done):
                    dst[chunk, base + t, :, at] = value

    a_chunks, b_chunks = (0, 1), (2, 3)
    greet(pltpu.get_barrier_semaphore())
    z_pieces(x_ref.at[0], z_in.at[0], 0, (1, n_z - 1))
    for hops in (2, 3):
        greet(ready_sem.at[hops - 2])
        z_pieces(x_ref.at[0], z_in.at[0], 0, (hops, n_z - hops))
    greet(ready_sem.at[2])
    z_pieces(x_ref.at[0], z_in.at[0], 0, (n_z // 2,))
    z_own(x_ref.at[0], z_in.at[0], 0)
    z_send(x_ref.at[1], z_in.at[1], 1)
    greet(ready_sem.at[3])
    for b in b_chunks:
        p_send(x_ref.at[b], p_in.at[b], 8 + b)

    table[...] = signs(lanes, lanes)

    for a, b in zip(a_chunks, b_chunks):
        arrived(p_in.at[b], 8 + b)
        combine(p_in.at[b], p_sum.at[b], n_p, p_len)
        p_send(p_sum.at[b], p_back.at[b], 12 + b)
        arrived(z_in.at[a], a)
        combine(z_in.at[a], z_sum.at[a], n_z, z_len)
        z_send(z_sum.at[a], z_back.at[a], 4 + a)

    for b in b_chunks:
        arrived(p_back.at[b], 12 + b)
    transform(p_back.at[pl.ds(2, 2)], local)
    for b in b_chunks:
        z_send(local.at[b - 2], z_in.at[b], b)

    for a in a_chunks:
        arrived(z_back.at[a], 4 + a)
        p_send(z_back.at[a], p_in.at[a], 8 + a)
    for a in a_chunks:
        arrived(p_in.at[a], 8 + a)
        combine(p_in.at[a], p_sum.at[a], n_p, p_len)
        p_send(p_sum.at[a], p_back.at[a], 12 + a)

    arrived(z_in.at[2], 2)
    combine(z_in.at[2], z_sum.at[2], n_z, z_len)
    z_send(z_sum.at[2], b_out.at[0], 6)

    for a in a_chunks:
        arrived(p_back.at[a], 12 + a)
    transform(p_back.at[pl.ds(0, 2)], a_out)

    arrived(z_in.at[3], 3)
    combine(z_in.at[3], z_sum.at[3], n_z, z_len)
    to_first_up = (z + 1) // n_z
    to_first_down = (lax.rem(z + n_z - 2, n_z) + 1) // n_z
    z_send(z_sum.at[3], b_out.at[1], 7, (2 - to_first_up, n_z - 2 + to_first_down, 1 + to_first_up, n_z - 1 - to_first_down))

    for b in b_chunks:
        arrived(b_out.at[b - 2], 4 + b)
    for c in range(CHUNKS):
        sent(z_in.at[c], z_len, c)
        sent(z_in.at[c], z_len, 4 + c)
        sent(p_in.at[c], p_len, 8 + c)
        sent(p_in.at[c], p_len, 12 + c)


def mix_kernel(scale, steps, a_ref, b_ref, o_ref, plus, minus, sem):
    chunks, blocks = a_ref.shape[:2]
    size = chunks * blocks // steps
    copies = []
    for i in range(steps):
        chunk, at = i * size // blocks, pl.ds(i * size % blocks, size)
        a, b = a_ref[chunk, at], b_ref[chunk, at]
        plus[chunk, at] = (a + b) * scale
        minus[chunk, at] = (a - b) * scale
        for half, made in enumerate((plus, minus)):
            copies.append(pltpu.make_async_copy(made.at[chunk, at], o_ref.at[half, chunk, at], sem.at[half, i]))
            copies[-1].start()
    for copy in copies:
        copy.wait()


def per_device(n_z, n_y, n_row, scale, query_weight):
    rows, lanes = query_weight.shape
    blocks = rows // CHUNKS // 8
    x = query_weight.reshape(CHUNKS, blocks, 8, lanes)
    half = pltpu.VMEM((2, blocks, 8, lanes), jnp.float32)
    full = pltpu.VMEM((CHUNKS, blocks, 8, lanes), jnp.float32)
    anywhere = pl.BlockSpec(memory_space=pl.ANY)
    a, b = pl.pallas_call(
        functools.partial(exchange_kernel, n_z, n_y, n_row),
        out_shape=(half, half),
        in_specs=[pl.BlockSpec(memory_space=pltpu.HBM)],
        out_specs=(pl.BlockSpec(memory_space=pltpu.VMEM),) * 2,
        scratch_shapes=[
            full, full, half, full, full, full, half,
            pltpu.VMEM((lanes, lanes), jnp.bfloat16),
            pltpu.SemaphoreType.DMA((4 * CHUNKS,)), pltpu.SemaphoreType.DMA((4 * CHUNKS,)), pltpu.SemaphoreType.REGULAR((4,)),
        ],
        compiler_params=pltpu.CompilerParams(collective_id=0, has_side_effects=True, vmem_limit_bytes=58 * 2**20),
        name="exchange",
    )(x)
    steps = 8
    a, b = (pltpu.with_memory_space_constraint(part, pltpu.VMEM) for part in (a, b))
    out = pl.pallas_call(
        functools.partial(mix_kernel, scale, steps),
        out_shape=jax.ShapeDtypeStruct((2, *half.shape), jnp.float32),
        in_specs=[pl.BlockSpec(memory_space=pltpu.VMEM)] * 2,
        out_specs=anywhere,
        scratch_shapes=[half, half, pltpu.SemaphoreType.DMA((2, steps))],
        compiler_params=pltpu.CompilerParams(vmem_limit_bytes=16 * 2**20),
        name="mix",
    )(a, b)
    return out.reshape(rows, lanes)


def solution(mesh):
    n_row, n_col = mesh.shape["row"], mesh.shape["col"]
    n_y = 4
    n_z = n_col // n_y

    def run(query_weight):
        scale = 1.0 / query_weight.shape[0]
        body = functools.partial(per_device, n_z, n_y, n_row, scale)
        return jax.shard_map(body, mesh=mesh, in_specs=(P("row", "col"),), out_specs=P("row", "col"), check_vma=False)(query_weight)

    return run
```

```python
import functools

import jax
import jax.numpy as jnp
from jax import lax
from jax.experimental import pallas as pl
from jax.experimental.pallas import tpu as pltpu
from jax.sharding import PartitionSpec as P

MESH = pl.DeviceIdType.MESH
LANES = 128
CHUNKS = 4
Z_ORDER = (4, 3, 5, 2, 6, 1, 7)
Z_EARLY = (1, 0, 2, 3)


def butterfly(values):
    values = list(values)
    half = 1
    while half < len(values):
        for base in range(0, len(values), 2 * half):
            for i in range(base, base + half):
                low, high = values[i], values[i + half]
                values[i], values[i + half] = low + high, low - high
        half *= 2
    return values


def signs(rows, cols):
    i = lax.broadcasted_iota(jnp.int32, (rows, cols), 0)
    j = lax.broadcasted_iota(jnp.int32, (rows, cols), 1)
    bits = jnp.bitwise_and(i, j)
    for shift in (8, 4, 2, 1):
        bits = jnp.bitwise_xor(bits, jnp.right_shift(bits, shift))
    return (1 - 2 * jnp.bitwise_and(bits, 1)).astype(jnp.float32).astype(jnp.bfloat16)


def split(value):
    high = value.astype(jnp.bfloat16)
    low = (value - high.astype(jnp.float32)).astype(jnp.bfloat16)
    return high, low


def exchange_kernel(n_z, n_y, n_row, x_ref, a_out, b_out, z_in, z_sum, z_back, p_in, p_sum, p_back, local, table, send_sem, recv_sem, ready_sem):
    row = lax.axis_index("row")
    col = lax.axis_index("col")
    z = col // n_y
    y = lax.rem(col, n_y)
    n_p = n_row * n_y
    p = row * n_y + y
    blocks, lanes = x_ref.shape[1], x_ref.shape[3]
    z_len, p_len = blocks // n_z, blocks // n_p

    def z_peer(step):
        k = lax.rem(z + step, n_z)
        return k, (row, k * n_y + y)

    def p_peer(step):
        k = lax.rem(p + step, n_p)
        return k, (k // n_y, z * n_y + lax.rem(k, n_y))

    x, core = row // 2, lax.rem(row, 2)
    n_x = n_row // 2
    neighbours = [z_peer(1)[1], z_peer(n_z - 1)[1]]
    neighbours += [(row, z * n_y + lax.rem(y + step, n_y)) for step in (1, n_y - 1)]
    neighbours += [(lax.rem(x + step, n_x) * 2 + core, col) for step in (1, n_x - 1)]
    neighbours += [(x * 2 + 1 - core, col)]

    def greet(semaphore):
        for device in neighbours:
            pl.semaphore_signal(semaphore, inc=1, device_id=device, device_id_type=MESH)
        pl.semaphore_wait(semaphore, len(neighbours))

    def z_piece(src, dst, slot, step):
        k, device = z_peer(step)
        pltpu.make_async_remote_copy(
            src_ref=src.at[pl.ds(k * z_len, z_len)], dst_ref=dst.at[pl.ds(z * z_len, z_len)],
            send_sem=send_sem.at[slot], recv_sem=recv_sem.at[slot], device_id=device, device_id_type=MESH,
        ).start()

    def z_own(src, dst, slot):
        mine = pl.ds(z * z_len, z_len)
        pltpu.make_async_copy(src.at[mine], dst.at[mine], recv_sem.at[slot]).start()

    def z_send(src, dst, slot):
        for step in Z_ORDER:
            z_piece(src, dst, slot, step)
        z_own(src, dst, slot)

    def z_send_early(src, dst, slot):
        for k in Z_EARLY:
            pl.when(z != k)(functools.partial(z_piece, src, dst, slot, lax.rem(k - z + n_z, n_z)))
        for step in Z_ORDER:
            late = lax.rem(z + step, n_z) >= len(Z_EARLY)
            pl.when(late)(functools.partial(z_piece, src, dst, slot, step))
        z_own(src, dst, slot)

    def p_send(src, dst, slot):
        mine = pl.ds(p * p_len, p_len)

        @pl.loop(1, n_p)
        def _(step):
            k, device = p_peer(step)
            pltpu.make_async_remote_copy(
                src_ref=src.at[pl.ds(k * p_len, p_len)], dst_ref=dst.at[mine],
                send_sem=send_sem.at[slot], recv_sem=recv_sem.at[slot], device_id=device, device_id_type=MESH,
            ).start()

        pltpu.make_async_copy(src.at[mine], dst.at[mine], recv_sem.at[slot]).start()

    def arrived(dst, slot):
        pltpu.make_async_copy(dst, dst, recv_sem.at[slot]).wait()

    def sent(ref, length, slot):
        part = ref.at[pl.ds(0, blocks - length)]
        pltpu.make_async_copy(part, part, send_sem.at[slot]).wait()

    def combine(src, dst, count, length):
        @pl.loop(0, length)
        def _(t):
            for lane in range(0, lanes, LANES):
                at = slice(lane, lane + LANES)
                done = butterfly([src[k * length + t, :, at] for k in range(count)])
                for k in range(count):
                    dst[k * length + t, :, at] = done[k]

    def transform(src, dst):
        size = 256
        groups = blocks * 8 // size
        step_blocks = size // 8

        @pl.loop(0, 2 * groups)
        def _(g):
            chunk, part = g // groups, lax.rem(g, groups)
            at = pl.ds(part * step_blocks, step_blocks)
            high, low = split(src[chunk, at].reshape(size, lanes))
            wide = table[...]
            value = jnp.dot(high, wide, preferred_element_type=jnp.float32) + jnp.dot(low, wide, preferred_element_type=jnp.float32)
            high, low = split(value)
            tall = table[0:size, 0:size]
            value = jnp.dot(tall, high, preferred_element_type=jnp.float32) + jnp.dot(tall, low, preferred_element_type=jnp.float32)
            dst[chunk, at] = value.reshape(step_blocks, 8, lanes)

        @pl.loop(0, step_blocks)
        def _(t):
            for lane in range(0, lanes, LANES):
                at = slice(lane, lane + LANES)
                places = [(chunk, part * step_blocks) for chunk in range(2) for part in range(groups)]
                done = butterfly([dst[chunk, base + t, :, at] for chunk, base in places])
                for (chunk, base), value in zip(places, done):
                    dst[chunk, base + t, :, at] = value

    a_chunks, b_chunks = (0, 1), (2, 3)
    greet(pltpu.get_barrier_semaphore())
    for hops in range(1, n_z // 2 + 1):
        if hops > 1:
            greet(ready_sem.at[hops - 2])
        for step in sorted({hops, n_z - hops}):
            z_piece(x_ref.at[0], z_in.at[0], 0, step)
    z_own(x_ref.at[0], z_in.at[0], 0)
    z_send(x_ref.at[1], z_in.at[1], 1)
    greet(ready_sem.at[3])
    for b in b_chunks:
        p_send(x_ref.at[b], p_in.at[b], 8 + b)

    table[...] = signs(lanes, lanes)

    for a, b in zip(a_chunks, b_chunks):
        arrived(p_in.at[b], 8 + b)
        combine(p_in.at[b], p_sum.at[b], n_p, p_len)
        p_send(p_sum.at[b], p_back.at[b], 12 + b)
        arrived(z_in.at[a], a)
        combine(z_in.at[a], z_sum.at[a], n_z, z_len)
        z_send(z_sum.at[a], z_back.at[a], 4 + a)

    for b in b_chunks:
        arrived(p_back.at[b], 12 + b)
    transform(p_back.at[pl.ds(2, 2)], local)
    for b in b_chunks:
        z_send(local.at[b - 2], z_in.at[b], b)

    for a in a_chunks:
        arrived(z_back.at[a], 4 + a)
        p_send(z_back.at[a], p_in.at[a], 8 + a)
    for a in a_chunks:
        arrived(p_in.at[a], 8 + a)
        combine(p_in.at[a], p_sum.at[a], n_p, p_len)
        p_send(p_sum.at[a], p_back.at[a], 12 + a)

    arrived(z_in.at[2], 2)
    combine(z_in.at[2], z_sum.at[2], n_z, z_len)
    z_send(z_sum.at[2], b_out.at[0], 6)

    for a in a_chunks:
        arrived(p_back.at[a], 12 + a)
    transform(p_back.at[pl.ds(0, 2)], a_out)

    arrived(z_in.at[3], 3)
    combine(z_in.at[3], z_sum.at[3], n_z, z_len)
    z_send_early(z_sum.at[3], b_out.at[1], 7)

    for b in b_chunks:
        arrived(b_out.at[b - 2], 4 + b)
    for c in range(CHUNKS):
        sent(z_in.at[c], z_len, c)
        sent(z_in.at[c], z_len, 4 + c)
        sent(p_in.at[c], p_len, 8 + c)
        sent(p_in.at[c], p_len, 12 + c)


def mix_kernel(scale, steps, a_ref, b_ref, o_ref, plus, minus, sem):
    chunks, blocks = a_ref.shape[:2]
    size = chunks * blocks // steps
    copies = []
    for i in range(steps):
        chunk, at = i * size // blocks, pl.ds(i * size % blocks, size)
        a, b = a_ref[chunk, at], b_ref[chunk, at]
        plus[chunk, at] = (a + b) * scale
        minus[chunk, at] = (a - b) * scale
        for half, made in enumerate((plus, minus)):
            copies.append(pltpu.make_async_copy(made.at[chunk, at], o_ref.at[half, chunk, at], sem.at[half, i]))
            copies[-1].start()
    for copy in copies:
        copy.wait()


def per_device(n_z, n_y, n_row, scale, query_weight):
    rows, lanes = query_weight.shape
    blocks = rows // CHUNKS // 8
    x = query_weight.reshape(CHUNKS, blocks, 8, lanes)
    half = pltpu.VMEM((2, blocks, 8, lanes), jnp.float32)
    full = pltpu.VMEM((CHUNKS, blocks, 8, lanes), jnp.float32)
    anywhere = pl.BlockSpec(memory_space=pl.ANY)
    a, b = pl.pallas_call(
        functools.partial(exchange_kernel, n_z, n_y, n_row),
        out_shape=(half, half),
        in_specs=[pl.BlockSpec(memory_space=pltpu.HBM)],
        out_specs=(pl.BlockSpec(memory_space=pltpu.VMEM),) * 2,
        scratch_shapes=[
            full, full, half, full, full, full, half,
            pltpu.VMEM((lanes, lanes), jnp.bfloat16),
            pltpu.SemaphoreType.DMA((4 * CHUNKS,)), pltpu.SemaphoreType.DMA((4 * CHUNKS,)), pltpu.SemaphoreType.REGULAR((4,)),
        ],
        compiler_params=pltpu.CompilerParams(collective_id=0, has_side_effects=True, vmem_limit_bytes=58 * 2**20),
        name="exchange",
    )(x)
    steps = 8
    a, b = (pltpu.with_memory_space_constraint(part, pltpu.VMEM) for part in (a, b))
    out = pl.pallas_call(
        functools.partial(mix_kernel, scale, steps),
        out_shape=jax.ShapeDtypeStruct((2, *half.shape), jnp.float32),
        in_specs=[pl.BlockSpec(memory_space=pltpu.VMEM)] * 2,
        out_specs=anywhere,
        scratch_shapes=[half, half, pltpu.SemaphoreType.DMA((2, steps))],
        compiler_params=pltpu.CompilerParams(vmem_limit_bytes=16 * 2**20),
        name="mix",
    )(a, b)
    return out.reshape(rows, lanes)


def solution(mesh):
    n_row, n_col = mesh.shape["row"], mesh.shape["col"]
    n_y = 4
    n_z = n_col // n_y

    def run(query_weight):
        scale = 1.0 / query_weight.shape[0]
        body = functools.partial(per_device, n_z, n_y, n_row, scale)
        return jax.shard_map(body, mesh=mesh, in_specs=(P("row", "col"),), out_specs=P("row", "col"), check_vma=False)(query_weight)

    return run
```
